32 devices in a mesh: seq: 16 (over z, x, core), wshard: 2 (over y).
Axes of the slice: x: 2, y: 2, z: 4, core: 2. Of those that a mesh axis runs over, the one named last changes fastest.
Arguments:
- block_input: float32 [2, 2048, 640], P('wshard', 'seq'), may hold values from -36 to 36
- attn_in: bfloat16 [640, 1536], P('wshard', 'seq'), may hold values from -0.25 to 0.25
- attn_out: bfloat16 [1024, 640], P('wshard', 'seq'), may hold values from -0.1875 to 0.1875
- ffn_in: bfloat16 [640, 4096], P('wshard', 'seq'), may hold values from -0.25 to 0.25
- ffn_out: bfloat16 [2048, 640], P('wshard', 'seq'), may hold values from -0.125 to 0.125
- norm_gains: bfloat16 [4, 640], P('wshard', 'seq'), may hold values from 0.25 to 1.75
- head_gains: bfloat16 [2, 256], P('wshard', 'seq'), may hold values from 0.25 to 1.75
- cotangent: float32 [2, 2048, 640], P('wshard', 'seq'), may hold values from -6 to 6
Outputs:
- block_output: float32 [2, 2048, 640], P('wshard', 'seq')
- input_grad: float32 [2, 2048, 640], P('wshard', 'seq')
- grad_attnin: float32 [640, 1536], P('wshard', 'seq')
- grad_attnout: float32 [1024, 640], P('wshard', 'seq')
- grad_ffnin: float32 [640, 4096], P('wshard', 'seq')
- grad_ffnout: float32 [2048, 640], P('wshard', 'seq')
- grad_norms: float32 [4, 640], P('wshard', 'seq')
- grad_heads: float32 [2, 256], P('wshard', 'seq')
The draws below stay inside these ranges and needn't reach their ends.
All inputs are finite; a program needn't handle non-finite values.
Results may differ from the reference program's by a relative error of at most 0.02.
Values may be sent and summed in bfloat16 or wider, within the bound.
A program may use at most 128 MiB of HBM per device.

```python
import math
import jax
import jax.numpy as jnp
from jax import lax

D = 640
NQ = 4
HD = 256
FF = 2048
WIN = 512
SEQ_LEN = 2048
SEQS = 2


def draw_block_input(key, part):
    key_base, key_rows, key_columns = jax.random.split(key, 3)
    row_scale = jnp.exp(jax.random.uniform(key_rows, (SEQS, SEQ_LEN, 1), jnp.float32, math.log(0.3), math.log(3.0)))
    column_scale = jnp.exp(jax.random.uniform(key_columns, (1, 1, D), jnp.float32, math.log(0.3), math.log(3.0)))
    base_values = jnp.clip(jax.random.normal(key_base, (SEQS, SEQ_LEN, D), jnp.float32), -4.0, 4.0)
    return (base_values * row_scale * column_scale).astype(jnp.float32)


def strengthened(values, key, source, target, parts, factor):
    def block_of(dim):
        return (jnp.arange(values.shape[dim]) // (values.shape[dim] // parts)).reshape((-1,) + (1,) * (values.ndim - 1 - dim))

    one_side = jax.random.permutation(key, parts)[block_of(target)]
    other_side = (block_of(target) + parts // 2) % parts
    return jnp.where((block_of(source) == one_side) | (block_of(source) == other_side), factor * values, values)


def shard_levels(stream_key, extent, pieces, smallest, high):
    level = 1.0
    for dim, blocks in pieces:
        draws = jax.random.uniform(jax.random.fold_in(jax.random.fold_in(stream_key, 6), dim), (blocks,), jnp.float32, smallest / len(pieces), high / len(pieces))
        level = level * jnp.repeat(jnp.exp(draws), extent[dim] // blocks).reshape((-1,) + (1,) * (len(extent) - 1 - dim))
    return level


def normal_values(stream_key, shape, scale, limit, shards=(), held_as=jnp.bfloat16):
    drawn = scale * jax.random.normal(stream_key, shape, jnp.float32)
    if shards:
        drawn = drawn * shard_levels(stream_key, shape, shards, -0.22, 0.18)
    return jnp.clip(drawn, -limit, limit).astype(held_as)


def heavy_noise(rng, dims, spread, reach, cuts, heavy, held_as=jnp.bfloat16):
    drawn = spread * jax.random.normal(rng, dims, jnp.float32)
    if cuts:
        drawn = drawn * shard_levels(rng, dims, cuts, -0.22, 0.18)
    return jnp.clip(strengthened(drawn, jax.random.fold_in(rng, 3), *heavy), -reach, reach).astype(held_as)


def setup_inputs(seed: int = 0) -> dict:
    arg_keys = jax.random.split(jax.random.key(seed), 9)
    block_input = draw_block_input(jax.random.fold_in(arg_keys[8], 71), 0)
    attn_in = normal_values(arg_keys[1], (D, (NQ + 2) * HD), D ** -0.5, 0.25, ((0, 2), (1, 16)))
    attn_out = normal_values(arg_keys[2], (NQ * HD, D), (NQ * HD) ** -0.5, 0.1875, ((0, 2), (1, 16)))
    ffn_in = normal_values(arg_keys[3], (D, 2 * FF), D ** -0.5, 0.25, ((0, 2), (1, 16)))
    ffn_out = normal_values(arg_keys[4], (FF, D), FF ** -0.5, 0.125, ((0, 2), (1, 16)))
    norm_gains = jnp.clip(1.0 + 0.15 * jax.random.normal(arg_keys[5], (4, D), jnp.float32), 0.25, 1.75).astype(jnp.bfloat16)
    head_gains = jnp.clip(1.0 + 0.15 * jax.random.normal(arg_keys[6], (2, HD), jnp.float32), 0.25, 1.75).astype(jnp.bfloat16)
    cotangent = heavy_noise(arg_keys[7], (SEQS, SEQ_LEN, D), 1.0, 6.0, ((0, 2), (1, 16)), (1, 2, 16, 2.0), jnp.float32)
    return {"block_input": block_input, "attn_in": attn_in, "attn_out": attn_out, "ffn_in": ffn_in, "ffn_out": ffn_out, "norm_gains": norm_gains, "head_gains": head_gains, "cotangent": cotangent}


EPS = 1e-06
QUERY_SCALE = 0.0625

def rms_forward(values, gain_row):
    inverse_rms = lax.rsqrt(lax.optimization_barrier(jnp.mean(values * values, axis=-1, keepdims=True)) + EPS)
    normed = values * inverse_rms
    return (normed * gain_row, normed, inverse_rms)

def rms_backward(normed, inverse_rms, gain_row, upstream):
    scaled = upstream * gain_row
    through = inverse_rms * (scaled - normed * lax.optimization_barrier(jnp.mean(scaled * normed, axis=-1, keepdims=True)))
    return (through, upstream * normed)

def rotary_tables(positions, head_size):
    half_size = head_size // 2
    inverse_freq = jnp.exp(jnp.arange(half_size, dtype=jnp.float32) * (-2.0 * math.log(10000.0) / head_size))
    angles = positions.astype(jnp.float32)[:, None] * inverse_freq[None, :]
    return (jnp.cos(angles), jnp.sin(angles))

def rotate(values, cosine_table, sine_table):
    half_size = values.shape[-1] // 2
    first_half = values[..., :half_size]
    second_half = values[..., half_size:]
    cosine_row = cosine_table[:, None, :]
    sine_row = sine_table[:, None, :]
    return jnp.concatenate([first_half * cosine_row - second_half * sine_row, second_half * cosine_row + first_half * sine_row], axis=-1)

def gated_gelu(gate_part, up_part):
    return jax.nn.gelu(gate_part, approximate=True) * up_part

def window_mask(query_positions, key_positions):
    query_column = query_positions[:, None]
    key_line = key_positions[None, :]
    return (key_line >= 0) & (key_line <= query_column) & (key_line > query_column - WIN)

def attend(query_block, key_block, value_block, allowed):
    scores = jnp.dot(query_block, key_block.T, preferred_element_type=jnp.float32)
    exponent = jnp.where(allowed, jnp.exp(scores), 0.0)
    totals = lax.optimization_barrier(jnp.sum(exponent, axis=-1, keepdims=True))
    probabilities = (exponent / totals).astype(jnp.bfloat16)
    mixture = jnp.dot(probabilities, value_block, preferred_element_type=jnp.float32).astype(jnp.bfloat16)
    return (mixture, jnp.log(totals))

def attend_back(query_block, key_block, value_block, allowed, mixture, log_totals, d_mixture):
    scores = jnp.dot(query_block, key_block.T, preferred_element_type=jnp.float32)
    probabilities = jnp.where(allowed, jnp.exp(scores - log_totals), 0.0)
    delta_row = lax.optimization_barrier(jnp.sum(d_mixture.astype(jnp.float32) * mixture.astype(jnp.float32), axis=-1, keepdims=True))
    d_probs = jnp.dot(d_mixture, value_block.T, preferred_element_type=jnp.float32)
    d_scores = (probabilities * (d_probs - delta_row)).astype(jnp.bfloat16)
    d_values = jnp.dot(probabilities.astype(jnp.bfloat16).T, d_mixture, preferred_element_type=jnp.float32)
    d_queries = jnp.dot(d_scores, key_block, preferred_element_type=jnp.float32)
    d_keys = jnp.dot(d_scores.T, query_block, preferred_element_type=jnp.float32)
    return (d_queries, d_keys, d_values)

def sequence_layer(tokens, upstream_out, whole_attnin, whole_attnout, whole_ffnin, whole_ffnout, gain_table, head_table):
    seq_rows = tokens.shape[0]
    positions = jnp.arange(seq_rows, dtype=jnp.int32)
    normed_in, unit_in, inverse_in = rms_forward(tokens, gain_table[0])
    hidden_in = normed_in.astype(jnp.bfloat16)
    projected = jnp.dot(hidden_in, whole_attnin, preferred_element_type=jnp.float32)
    query_raw = projected[:, :NQ * HD].reshape(seq_rows, NQ, HD)
    key_raw = projected[:, NQ * HD:(NQ + 1) * HD].reshape(seq_rows, 1, HD)
    value_raw = projected[:, (NQ + 1) * HD:]
    query_norm, query_unit, query_inverse = rms_forward(query_raw, head_table[0])
    key_norm, key_unit, key_inverse = rms_forward(key_raw, head_table[1])
    cosine_table, sine_table = rotary_tables(positions, HD)
    query_rot = (rotate(query_norm, cosine_table, sine_table) * QUERY_SCALE).astype(jnp.bfloat16).reshape(seq_rows * NQ, HD)
    key_rot = rotate(key_norm, cosine_table, sine_table).reshape(seq_rows, HD).astype(jnp.bfloat16)
    value_part = value_raw.astype(jnp.bfloat16)
    block_rows = math.gcd(512, seq_rows)
    block_count = seq_rows // block_rows
    key_padded = jnp.concatenate([jnp.zeros((WIN, HD), jnp.bfloat16), key_rot], axis=0)
    value_padded = jnp.concatenate([jnp.zeros((WIN, HD), jnp.bfloat16), value_part], axis=0)

    def block_inputs(block_index):
        start_row = (block_index * block_rows).astype(jnp.int32)
        query_block = lax.dynamic_slice_in_dim(query_rot, (start_row * NQ).astype(jnp.int32), block_rows * NQ, 0)
        key_block = lax.dynamic_slice_in_dim(key_padded, start_row, block_rows + WIN, 0)
        value_block = lax.dynamic_slice_in_dim(value_padded, start_row, block_rows + WIN, 0)
        query_positions = jnp.repeat(start_row + jnp.arange(block_rows, dtype=jnp.int32), NQ)
        key_positions = start_row - WIN + jnp.arange(block_rows + WIN, dtype=jnp.int32)
        return (start_row, query_block, key_block, value_block, window_mask(query_positions, key_positions))

    def forward_block(block_index):
        start_row, query_block, key_block, value_block, allowed = block_inputs(block_index)
        return attend(query_block, key_block, value_block, allowed)
    block_ids = jnp.arange(block_count, dtype=jnp.int32)
    mixture, log_totals = lax.map(forward_block, block_ids)
    attended = mixture.reshape(seq_rows, NQ * HD)
    attn_proj = jnp.dot(attended, whole_attnout, preferred_element_type=jnp.float32)
    post_attn, unit_attn, inverse_attn = rms_forward(attn_proj, gain_table[1])
    middle = tokens + post_attn
    normed_mid, unit_mid, inverse_mid = rms_forward(middle, gain_table[2])
    hidden_mid = normed_mid.astype(jnp.bfloat16)
    gate_up = jnp.dot(hidden_mid, whole_ffnin, preferred_element_type=jnp.float32)
    activated, gelu_back = jax.vjp(gated_gelu, gate_up[:, :FF], gate_up[:, FF:])
    activated_bf = activated.astype(jnp.bfloat16)
    ffn_proj = jnp.dot(activated_bf, whole_ffnout, preferred_element_type=jnp.float32)
    post_ffn, unit_ffn, inverse_ffn = rms_forward(ffn_proj, gain_table[3])
    output = middle + post_ffn
    d_ffnproj, gain_four = rms_backward(unit_ffn, inverse_ffn, gain_table[3], upstream_out)
    d_ffn_bf = d_ffnproj.astype(jnp.bfloat16)
    grad_ffnout = jnp.dot(activated_bf.T, d_ffn_bf, preferred_element_type=jnp.float32)
    d_activated = jnp.dot(d_ffn_bf, whole_ffnout.T, preferred_element_type=jnp.float32)
    d_gate, d_up = gelu_back(d_activated)
    d_gateup = jnp.concatenate([d_gate, d_up], axis=1).astype(jnp.bfloat16)
    grad_ffnin = jnp.dot(hidden_mid.T, d_gateup, preferred_element_type=jnp.float32)
    d_normmid = jnp.dot(d_gateup, whole_ffnin.T, preferred_element_type=jnp.float32)
    d_middle_part, gain_three = rms_backward(unit_mid, inverse_mid, gain_table[2], d_normmid)
    d_middle = upstream_out + d_middle_part
    d_attnproj, gain_two = rms_backward(unit_attn, inverse_attn, gain_table[1], d_middle)
    d_attn_bf = d_attnproj.astype(jnp.bfloat16)
    grad_attnout = jnp.dot(attended.T, d_attn_bf, preferred_element_type=jnp.float32)
    d_mixed = jnp.dot(d_attn_bf, whole_attnout.T, preferred_element_type=jnp.float32).astype(jnp.bfloat16)
    d_mixed = d_mixed.reshape(block_count, block_rows * NQ, HD)

    def backward_block(carried, block_index):
        start_row, query_block, key_block, value_block, allowed = block_inputs(block_index)
        d_queries, d_keys, d_values = attend_back(query_block, key_block, value_block, allowed, mixture[block_index], log_totals[block_index], d_mixed[block_index])
        update = jnp.concatenate([d_keys, d_values], axis=1)
        current = lax.dynamic_slice_in_dim(carried, start_row, block_rows + WIN, 0)
        carried = lax.dynamic_update_slice_in_dim(carried, current + update, start_row, 0)
        return (carried, d_queries)
    pair_grad, d_queries = lax.scan(backward_block, jnp.zeros((WIN + seq_rows, 2 * HD), jnp.float32), block_ids)
    pair_grad = pair_grad[WIN:]
    d_keynorm = rotate(pair_grad[:, :HD].reshape(seq_rows, 1, HD), cosine_table, -sine_table)
    d_keyraw, gain_key = rms_backward(key_unit, key_inverse, head_table[1], d_keynorm)
    d_queryrot = d_queries.reshape(seq_rows, NQ, HD) * QUERY_SCALE
    d_querynorm = rotate(d_queryrot, cosine_table, -sine_table)
    d_queryraw, gain_query = rms_backward(query_unit, query_inverse, head_table[0], d_querynorm)
    d_projected = jnp.concatenate([d_queryraw.reshape(seq_rows, NQ * HD), d_keyraw.reshape(seq_rows, HD), pair_grad[:, HD:]], axis=1).astype(jnp.bfloat16)
    grad_attnin = jnp.dot(hidden_in.T, d_projected, preferred_element_type=jnp.float32)
    d_normin = jnp.dot(d_projected, whole_attnin.T, preferred_element_type=jnp.float32)
    d_tokens_part, gain_one = rms_backward(unit_in, inverse_in, gain_table[0], d_normin)
    input_grad = d_middle + d_tokens_part
    grad_norms = jnp.stack([lax.optimization_barrier(jnp.sum(gain_one, axis=0)), lax.optimization_barrier(jnp.sum(gain_two, axis=0)), lax.optimization_barrier(jnp.sum(gain_three, axis=0)), lax.optimization_barrier(jnp.sum(gain_four, axis=0))])
    grad_heads = jnp.stack([lax.optimization_barrier(jnp.sum(gain_query.reshape(-1, HD), axis=0)), lax.optimization_barrier(jnp.sum(gain_key.reshape(-1, HD), axis=0))])
    return (output, input_grad, (grad_attnin, grad_attnout, grad_ffnin, grad_ffnout, grad_norms, grad_heads))

def reference(block_input, attn_in, attn_out, ffn_in, ffn_out, norm_gains, head_gains, cotangent):
    gain_table = norm_gains.astype(jnp.float32)
    head_table = head_gains.astype(jnp.float32)
    outputs = []
    input_grads = []
    gradients = None
    for sequence_index in range(SEQS):
        output, input_grad, local_grads = sequence_layer(block_input[sequence_index], cotangent[sequence_index], attn_in, attn_out, ffn_in, ffn_out, gain_table, head_table)
        outputs.append(output)
        input_grads.append(input_grad)
        if gradients is None:
            gradients = local_grads
        else:
            gradients = tuple((first_term + second_term for first_term, second_term in zip(gradients, local_grads)))
    return (jnp.stack(outputs), jnp.stack(input_grads), gradients[0], gradients[1], gradients[2], gradients[3], gradients[4], gradients[5])
```

```python
import math

import jax
import jax.numpy as jnp
from jax import lax
from jax.experimental import pallas as pl
from jax.experimental.pallas import tpu as pltpu
from jax.sharding import PartitionSpec as P

NQ = 4
HD = 256
FF = 2048
WIN = 512


EPS = 1e-06
QUERY_SCALE = 0.0625


def shifted(value, axis, steps):
    count = lax.axis_size(axis)
    initial, last = (max(0, -steps), min(count, count - steps))
    return lax.ppermute(value, axis, [(source, source + steps) for source in range(initial, last)])


def rms_forward(values, gain_row):
    inverse_rms = lax.rsqrt(jnp.mean(values * values, axis=-1, keepdims=True) + EPS)
    normed = values * inverse_rms
    return (normed * gain_row, normed, inverse_rms)


def rms_backward(normed, inverse_rms, gain_row, upstream):
    scaled = upstream * gain_row
    through = inverse_rms * (scaled - normed * jnp.mean(scaled * normed, axis=-1, keepdims=True))
    return (through, upstream * normed)


def rotary_tables(positions, head_size):
    half_size = head_size // 2
    inverse_freq = jnp.exp(
        jnp.arange(half_size, dtype=jnp.float32) * (-2.0 * math.log(10000.0) / head_size)
    )
    angles = positions.astype(jnp.float32)[:, None] * inverse_freq[None, :]
    return (jnp.cos(angles), jnp.sin(angles))


def rotate(values, cosine_table, sine_table):
    half_size = values.shape[-1] // 2
    first_half = values[..., :half_size]
    second_half = values[..., half_size:]
    cosine_row = cosine_table[:, None, :]
    sine_row = sine_table[:, None, :]
    return jnp.concatenate(
        [
            first_half * cosine_row - second_half * sine_row,
            second_half * cosine_row + first_half * sine_row,
        ],
        axis=-1,
    )


def gated_gelu(gate_part, up_part):
    return jax.nn.gelu(gate_part, approximate=True) * up_part


def window_mask(query_positions, key_positions):
    query_column = query_positions[:, None]
    key_line = key_positions[None, :]
    return (key_line >= 0) & (key_line <= query_column) & (key_line > query_column - WIN)


def attend(query_block, key_block, value_block, allowed):
    scores = jnp.dot(query_block, key_block.T, preferred_element_type=jnp.float32)
    exponent = jnp.where(allowed, jnp.exp(scores), 0.0)
    totals = jnp.sum(exponent, axis=-1, keepdims=True)
    probabilities = (exponent / totals).astype(jnp.bfloat16)
    mixture = jnp.dot(probabilities, value_block, preferred_element_type=jnp.float32).astype(
        jnp.bfloat16
    )
    return (mixture, jnp.log(totals))


def attend_back(query_block, key_block, value_block, allowed, mixture, log_totals, d_mixture):
    scores = jnp.dot(query_block, key_block.T, preferred_element_type=jnp.float32)
    probabilities = jnp.where(allowed, jnp.exp(scores - log_totals), 0.0)
    delta_row = jnp.sum(
        d_mixture.astype(jnp.float32) * mixture.astype(jnp.float32), axis=-1, keepdims=True
    )
    d_probs = jnp.dot(d_mixture, value_block.T, preferred_element_type=jnp.float32)
    d_scores = (probabilities * (d_probs - delta_row)).astype(jnp.bfloat16)
    d_values = jnp.dot(
        probabilities.astype(jnp.bfloat16).T, d_mixture, preferred_element_type=jnp.float32
    )
    d_queries = jnp.dot(d_scores, key_block, preferred_element_type=jnp.float32)
    d_keys = jnp.dot(d_scores.T, query_block, preferred_element_type=jnp.float32)
    return (d_queries, d_keys, d_values)


MESH = pl.DeviceIdType.MESH


def axis_bits(count):
    return count.bit_length() - 1


def coordinates(bits):
    place = lax.axis_index("seq")
    values = [lax.axis_index("wshard")]
    for bit in range(bits - 1, -1, -1):
        values.append(lax.rem(lax.div(place, 2**bit), 2))
    return values


def partner(dim, coords, bits):
    if dim == 0:
        return (lax.axis_index("seq"), 1 - coords[0])
    step = 2 ** (bits - dim)
    return (lax.axis_index("seq") + (1 - 2 * coords[dim]) * step, lax.axis_index("wshard"))


def greet(coords, bits):
    barrier = pltpu.get_barrier_semaphore()
    for dim in range(bits + 1):
        pl.semaphore_signal(
            barrier, inc=1, device_id=partner(dim, coords, bits), device_id_type=MESH
        )
    pl.semaphore_wait(barrier, bits + 1)


def scatter_order(bits, flipped):
    middle = [0, bits - 1] if flipped else [bits - 1, 0]
    return [bits] + middle + list(range(bits - 2, 0, -1))


class Piece:
    def __init__(self, ref, rows, lanes, wdim, lane_part, flipped, dtype=jnp.bfloat16):
        self.ref, self.rows, self.lanes, self.wdim = ref, rows, lanes, wdim
        self.lane_part, self.flipped, self.dtype = lane_part, flipped, dtype

    def slices(self, picks, bits, base_lane):
        index = []
        rows, lanes = pl.ds(0, self.rows), pl.ds(base_lane, self.lanes)
        if 0 in picks:
            pick = picks[0]
            if self.wdim == "lead":
                index.append(slice(None) if pick is None else pick)
            elif self.wdim == "rows":
                if pick is None:
                    rows = pl.ds(0, 2 * self.rows)
                else:
                    rows = pl.ds(pl.multiple_of(pick * self.rows, self.rows), self.rows)
            else:
                if pick is None:
                    lanes = pl.ds(0, 2 * self.lanes)
                else:
                    lanes = pl.ds(pl.multiple_of(pick * self.lanes, self.lanes), self.lanes)
        for dim in range(1, bits + 1):
            if dim in picks:
                pick = picks[dim]
                index.append(slice(None) if pick is None else pick)
        return tuple(index) + (rows, lanes)

    def shape(self, dims):
        rows, lanes, lead = self.rows, self.lanes, []
        for dim in sorted(dims):
            if dim > 0 or self.wdim == "lead":
                lead.append(2)
            elif self.wdim == "rows":
                rows *= 2
            else:
                lanes *= 2
        return tuple(lead) + (rows, lanes)


def gather_pieces(shapes):
    out = []
    for number, (rows, lanes, wdim, parts) in enumerate(shapes):
        for part in range(parts):
            out.append(
                Piece(number, rows, lanes // parts, wdim, part, (part == 1) or (number % 2 == 1))
            )
    return out


def gather_kernel(pieces, bits, count, *refs):
    blocks, outs = refs[:count], refs[count : 2 * count]
    send_sems, recv_sems, local_sems = refs[2 * count :]
    coords = coordinates(bits)
    own = {dim: coords[dim] for dim in range(bits + 1)}
    local = []
    for number, piece in enumerate(pieces):
        lane = piece.lane_part * piece.lanes
        copy = pltpu.make_async_copy(
            blocks[piece.ref].at[:, pl.ds(lane, piece.lanes)],
            outs[piece.ref].at[piece.slices(own, bits, lane)],
            local_sems.at[number],
        )
        copy.start()
        local.append(copy)
    greet(coords, bits)
    orders = [scatter_order(bits, piece.flipped)[::-1] for piece in pieces]
    held = [dict(own) for _ in pieces]
    last = list(local)
    sent = []
    for stage in range(bits + 1):
        for number, piece in enumerate(pieces):
            if stage == 0:
                last[number].wait()
            else:
                last[number].wait_recv()
            dim = orders[number][stage]
            lane = piece.lane_part * piece.lanes
            region = outs[piece.ref].at[piece.slices(held[number], bits, lane)]
            copy = pltpu.make_async_remote_copy(
                src_ref=region,
                dst_ref=region,
                send_sem=send_sems.at[number, stage],
                recv_sem=recv_sems.at[number, stage],
                device_id=partner(dim, coords, bits),
                device_id_type=MESH,
            )
            copy.start()
            held[number][dim] = None
            last[number] = copy
            sent.append(copy)
    for number in range(len(pieces)):
        last[number].wait_recv()
    for copy in sent:
        copy.wait_send()


def gather_blocks(blocks, shapes, bits):
    pieces = gather_pieces(shapes)
    full = []
    for (rows, lanes, wdim, parts), block in zip(shapes, blocks):
        whole = Piece(0, rows, lanes, wdim, 0, False).shape(range(bits + 1))
        full.append(jax.ShapeDtypeStruct(whole, block.dtype))
    count = len(blocks)
    return pl.pallas_call(
        lambda *refs: gather_kernel(pieces, bits, count, *refs),
        out_shape=full,
        in_specs=[pl.BlockSpec(memory_space=pltpu.VMEM)] * count,
        out_specs=[pl.BlockSpec(memory_space=pl.ANY)] * count,
        scratch_shapes=[
            pltpu.SemaphoreType.DMA((len(pieces), bits + 1)),
            pltpu.SemaphoreType.DMA((len(pieces), bits + 1)),
            pltpu.SemaphoreType.DMA((len(pieces),)),
        ],
        compiler_params=pltpu.CompilerParams(collective_id=0, has_side_effects=True),
        name="gather_weights",
    )(*blocks)


def scatter_kernel(pieces, bits, count, *refs):
    grads, outs = refs[:count], refs[count : 2 * count]
    send_sems, recv_sems = refs[-2:]
    slots = refs[2 * count : -2]
    coords = coordinates(bits)
    greet(coords, bits)
    orders = [scatter_order(bits, piece.flipped) for piece in pieces]
    left = [{dim: None for dim in range(bits + 1)} for _ in pieces]
    current = [grads[piece.ref] for piece in pieces]
    lanes_at = [piece.lane_part * piece.lanes for piece in pieces]
    pending = [None] * len(pieces)
    sent = []

    def finish(number, stage):
        copy, keep = pending[number]
        copy.wait_recv()
        slot = slots[number * (bits + 1) + stage]
        mine = current[number][keep].astype(jnp.float32)
        total = mine + slot[...].astype(jnp.float32)
        current[number], lanes_at[number] = slot, 0
        return slot, total

    for stage in range(bits + 1):
        for number, piece in enumerate(pieces):
            if stage > 0:
                slot, total = finish(number, stage - 1)
                slot[...] = total.astype(slot.dtype)
            dim = orders[number][stage]
            picks = dict(left[number])
            picks[dim] = 1 - coords[dim]
            give = piece.slices(picks, bits, lanes_at[number])
            picks[dim] = coords[dim]
            keep = piece.slices(picks, bits, lanes_at[number])
            copy = pltpu.make_async_remote_copy(
                src_ref=current[number].at[give],
                dst_ref=slots[number * (bits + 1) + stage],
                send_sem=send_sems.at[number, stage],
                recv_sem=recv_sems.at[number, stage],
                device_id=partner(dim, coords, bits),
                device_id_type=MESH,
            )
            copy.start()
            del left[number][dim]
            pending[number] = (copy, keep)
            sent.append(copy)
    for number, piece in enumerate(pieces):
        slot, total = finish(number, bits)
        lane = piece.lane_part * piece.lanes
        outs[piece.ref][:, pl.ds(lane, piece.lanes)] = total
    for copy in sent:
        copy.wait_send()


def scatter_blocks(grads, shapes, bits):
    pieces = gather_pieces(shapes)
    slots = []
    for piece in pieces:
        dims = list(range(bits + 1))
        for dim in scatter_order(bits, piece.flipped):
            dims.remove(dim)
            slots.append(pltpu.VMEM(piece.shape(dims), grads[piece.ref].dtype))
    count = len(grads)
    return pl.pallas_call(
        lambda *refs: scatter_kernel(pieces, bits, count, *refs),
        out_shape=[
            jax.ShapeDtypeStruct((rows, lanes), jnp.float32) for rows, lanes, _, _ in shapes
        ],
        in_specs=[pl.BlockSpec(memory_space=pltpu.VMEM)] * count,
        out_specs=[pl.BlockSpec(memory_space=pltpu.VMEM)] * count,
        scratch_shapes=slots
        + [
            pltpu.SemaphoreType.DMA((len(pieces), bits + 1)),
            pltpu.SemaphoreType.DMA((len(pieces), bits + 1)),
        ],
        compiler_params=pltpu.CompilerParams(
            collective_id=1, has_side_effects=True, vmem_limit_bytes=60 * 1024 * 1024
        ),
        name="scatter_grads",
    )(*grads)


def shards(block_input, attn_in, attn_out, ffn_in, ffn_out, norm_gains, head_gains, cotangent):
    seq_count = lax.axis_size("seq")
    bits = axis_bits(seq_count)
    gain_rows, gain_cols = norm_gains.shape
    head_rows, head_cols = head_gains.shape
    width = block_input.shape[-1]
    gain_block = jnp.concatenate(
        [
            jnp.pad(norm_gains, ((0, 0), (0, 128 - gain_cols))),
            jnp.pad(head_gains, ((0, 16 - gain_rows - head_rows), (0, 128 - head_cols))),
        ],
        axis=0,
    )
    wide = ffn_in.shape[1] % 256 == 0
    up_block = ffn_in if wide else ffn_in.T
    in_block, out_block, down_block = (attn_in.T, attn_out.T, ffn_out.T)
    layouts = (
        (*in_block.shape, "lead", 1),
        (*out_block.shape, "lanes", 1),
        (*up_block.shape, "rows", 2) if wide else (*up_block.shape, "lead", 1),
        (*down_block.shape, "lanes", 1),
    )
    gathered = gather_blocks(
        (in_block, out_block, up_block, down_block, gain_block),
        layouts + ((16, 128, "lead", 1),),
        bits,
    )
    in_halves = gathered[0].reshape(2, -1, in_block.shape[1])
    attnin_t = jnp.concatenate([in_halves[0], in_halves[1]], axis=1)
    attnout_t = gathered[1].reshape(width, -1)
    if wide:
        whole_ffnin = (
            gathered[2]
            .reshape(seq_count, width, up_block.shape[1])
            .transpose(1, 0, 2)
            .reshape(width, -1)
        )
    else:
        up_halves = gathered[2].reshape(2, -1, up_block.shape[1])
        whole_ffnin = jnp.concatenate([up_halves[0], up_halves[1]], axis=1).T
    ffnout_t = gathered[3].reshape(width, -1)
    gain_all = gathered[4].reshape(2, seq_count, 16, 128)
    whole_norms = (
        gain_all[:, :, :gain_rows, :gain_cols].transpose(0, 2, 1, 3).reshape(2 * gain_rows, -1)
    )
    whole_heads = (
        gain_all[:, :, gain_rows : gain_rows + head_rows, :head_cols]
        .transpose(0, 2, 1, 3)
        .reshape(2 * head_rows, -1)
    )
    gain_table = whole_norms.astype(jnp.float32)
    head_table = whole_heads.astype(jnp.float32)
    tokens = block_input[0]
    upstream_out = cotangent[0]
    row_count = tokens.shape[0]
    hop_count = (WIN - 1) // row_count + 1
    positions = lax.axis_index("seq") * row_count + jnp.arange(row_count, dtype=jnp.int32)
    normed_in, unit_in, inverse_in = rms_forward(tokens, gain_table[0])
    hidden_in = normed_in.astype(jnp.bfloat16)
    projected = jnp.dot(hidden_in, attnin_t.T, preferred_element_type=jnp.float32)
    query_raw = projected[:, : NQ * HD].reshape(row_count, NQ, HD)
    key_raw = projected[:, NQ * HD : (NQ + 1) * HD].reshape(row_count, 1, HD)
    value_raw = projected[:, (NQ + 1) * HD :]
    query_norm, query_unit, query_inverse = rms_forward(query_raw, head_table[0])
    key_norm, key_unit, key_inverse = rms_forward(key_raw, head_table[1])
    cosine_table, sine_table = rotary_tables(positions, HD)
    query_rot = (
        (rotate(query_norm, cosine_table, sine_table) * QUERY_SCALE)
        .astype(jnp.bfloat16)
        .reshape(row_count * NQ, HD)
    )
    key_rot = rotate(key_norm, cosine_table, sine_table).reshape(row_count, HD).astype(jnp.bfloat16)
    own_pair = jnp.concatenate([key_rot, value_raw.astype(jnp.bfloat16)], axis=1)
    earlier = []
    for distance in range(hop_count, 0, -1):
        earlier.append(shifted(own_pair, "seq", distance))
    window_pair = jnp.concatenate(earlier + [own_pair], axis=0)
    keys_all = window_pair[:, :HD]
    values_all = window_pair[:, HD:]
    key_positions = (
        positions[0]
        - hop_count * row_count
        + jnp.arange((hop_count + 1) * row_count, dtype=jnp.int32)
    )
    allowed = window_mask(jnp.repeat(positions, NQ), key_positions)
    mixture, log_totals = attend(query_rot, keys_all, values_all, allowed)
    attended = mixture.reshape(row_count, NQ * HD)
    attn_proj = jnp.dot(attended, attnout_t.T, preferred_element_type=jnp.float32)
    post_attn, unit_attn, inverse_attn = rms_forward(attn_proj, gain_table[1])
    middle = tokens + post_attn
    normed_mid, unit_mid, inverse_mid = rms_forward(middle, gain_table[2])
    hidden_mid = normed_mid.astype(jnp.bfloat16)
    gate_up = jnp.dot(hidden_mid, whole_ffnin, preferred_element_type=jnp.float32)
    activated, gelu_back = jax.vjp(gated_gelu, gate_up[:, :FF], gate_up[:, FF:])
    activated_bf = activated.astype(jnp.bfloat16)
    ffn_proj = jnp.dot(activated_bf, ffnout_t.T, preferred_element_type=jnp.float32)
    post_ffn, unit_ffn, inverse_ffn = rms_forward(ffn_proj, gain_table[3])
    output = middle + post_ffn
    d_ffnproj, gain_four = rms_backward(unit_ffn, inverse_ffn, gain_table[3], upstream_out)
    d_ffn_bf = d_ffnproj.astype(jnp.bfloat16)
    grad_ffnout = jnp.dot(d_ffn_bf.T, activated_bf, preferred_element_type=jnp.float32)
    d_activated = jnp.dot(d_ffn_bf, ffnout_t, preferred_element_type=jnp.float32)
    d_gate, d_up = gelu_back(d_activated)
    d_gateup = jnp.concatenate([d_gate, d_up], axis=1).astype(jnp.bfloat16)
    grad_ffnin = jnp.dot(hidden_mid.T, d_gateup, preferred_element_type=jnp.float32)
    d_normmid = jnp.dot(d_gateup, whole_ffnin.T, preferred_element_type=jnp.float32)
    d_middle_part, gain_three = rms_backward(unit_mid, inverse_mid, gain_table[2], d_normmid)
    d_middle = upstream_out + d_middle_part
    d_attnproj, gain_two = rms_backward(unit_attn, inverse_attn, gain_table[1], d_middle)
    d_attn_bf = d_attnproj.astype(jnp.bfloat16)
    grad_attnout = jnp.dot(d_attn_bf.T, attended, preferred_element_type=jnp.float32)
    d_mixed = jnp.dot(d_attn_bf, attnout_t, preferred_element_type=jnp.float32).astype(
        jnp.bfloat16
    )
    d_mixed = d_mixed.reshape(row_count * NQ, HD)
    d_queries, d_keys, d_values = attend_back(
        query_rot, keys_all, values_all, allowed, mixture, log_totals, d_mixed
    )
    pair_all = jnp.concatenate([d_keys, d_values], axis=1)
    pair_grad = pair_all[hop_count * row_count :]
    for distance in range(1, hop_count + 1):
        start_row = (hop_count - distance) * row_count
        pair_grad = pair_grad + shifted(
            pair_all[start_row : start_row + row_count].astype(jnp.bfloat16), "seq", -distance
        ).astype(jnp.float32)
    d_keynorm = rotate(pair_grad[:, :HD].reshape(row_count, 1, HD), cosine_table, -sine_table)
    d_keyraw, gain_key = rms_backward(key_unit, key_inverse, head_table[1], d_keynorm)
    d_queryrot = d_queries.reshape(row_count, NQ, HD) * QUERY_SCALE
    d_querynorm = rotate(d_queryrot, cosine_table, -sine_table)
    d_queryraw, gain_query = rms_backward(query_unit, query_inverse, head_table[0], d_querynorm)
    d_projected = jnp.concatenate(
        [
            d_queryraw.reshape(row_count, NQ * HD),
            d_keyraw.reshape(row_count, HD),
            pair_grad[:, HD:],
        ],
        axis=1,
    ).astype(jnp.bfloat16)
    half_width = in_block.shape[1]
    grad_attnin = jnp.stack(
        [
            jnp.dot(
                d_projected.T,
                hidden_in[:, half * half_width : (half + 1) * half_width],
                preferred_element_type=jnp.float32,
            )
            for half in range(2)
        ]
    )
    d_normin = jnp.dot(d_projected, attnin_t, preferred_element_type=jnp.float32)
    d_tokens_part, gain_one = rms_backward(unit_in, inverse_in, gain_table[0], d_normin)
    input_grad = d_middle + d_tokens_part
    grad_norms = jnp.stack(
        [
            jnp.sum(gain_one, axis=0),
            jnp.sum(gain_two, axis=0),
            jnp.sum(gain_three, axis=0),
            jnp.sum(gain_four, axis=0),
        ]
    )
    grad_heads = jnp.stack(
        [jnp.sum(gain_query.reshape(-1, HD), axis=0), jnp.sum(gain_key.reshape(-1, HD), axis=0)]
    )
    bit_dims = (2,) * bits
    gain_sums = jnp.concatenate(
        [
            jnp.pad(
                grad_norms.reshape(2, gain_rows, seq_count, gain_cols).transpose(0, 2, 1, 3),
                ((0, 0), (0, 0), (0, 0), (0, 128 - gain_cols)),
            ),
            jnp.pad(
                grad_heads.reshape(2, head_rows, seq_count, head_cols).transpose(0, 2, 1, 3),
                ((0, 0), (0, 0), (0, 8 - gain_rows - head_rows), (0, 128 - head_cols)),
            ),
        ],
        axis=2,
    )
    up_sums = grad_ffnin.astype(jnp.bfloat16)
    if wide:
        up_sums = (
            up_sums.reshape(width, seq_count, -1)
            .transpose(1, 0, 2)
            .reshape(bit_dims + (width, up_block.shape[1]))
        )
    else:
        up_sums = up_sums.reshape(2, up_block.shape[1], -1).transpose(0, 2, 1)
        up_sums = up_sums.reshape((2,) + bit_dims + up_block.shape)
    reduced = scatter_blocks(
        (
            grad_attnin.astype(jnp.bfloat16).reshape((2,) + bit_dims + in_block.shape),
            grad_attnout.astype(jnp.bfloat16).reshape(bit_dims + (out_block.shape[0], -1)),
            up_sums,
            grad_ffnout.astype(jnp.bfloat16).reshape(bit_dims + (down_block.shape[0], -1)),
            gain_sums.reshape((2,) + bit_dims + (8, 128)),
        ),
        layouts + ((8, 128, "lead", 1),),
        bits,
    )
    return (
        output[None],
        input_grad[None],
        reduced[0].T,
        reduced[1].T,
        reduced[2] if wide else reduced[2].T,
        reduced[3].T,
        reduced[4][:gain_rows, :gain_cols],
        reduced[4][gain_rows : gain_rows + head_rows, :head_cols],
    )


def solution(mesh):
    in_specs = (
        P("wshard", "seq", None),
        P("wshard", "seq"),
        P("wshard", "seq"),
        P("wshard", "seq"),
        P("wshard", "seq"),
        P("wshard", "seq"),
        P("wshard", "seq"),
        P("wshard", "seq", None),
    )
    out_specs = (
        P("wshard", "seq", None),
        P("wshard", "seq", None),
        P("wshard", "seq"),
        P("wshard", "seq"),
        P("wshard", "seq"),
        P("wshard", "seq"),
        P("wshard", "seq"),
        P("wshard", "seq"),
    )
    return jax.shard_map(shards, mesh=mesh, in_specs=in_specs, out_specs=out_specs, check_vma=False)
```

```python
import math

import jax
import jax.numpy as jnp
from jax import lax
from jax.experimental import pallas as pl
from jax.experimental.pallas import tpu as pltpu
from jax.sharding import PartitionSpec as P

NQ = 4
HD = 256
FF = 2048
WIN = 512


EPS = 1e-06
QUERY_SCALE = 0.0625


def shifted(value, axis, steps):
    count = lax.axis_size(axis)
    initial, last = (max(0, -steps), min(count, count - steps))
    return lax.ppermute(value, axis, [(source, source + steps) for source in range(initial, last)])


def rms_forward(values, gain_row):
    inverse_rms = lax.rsqrt(jnp.mean(values * values, axis=-1, keepdims=True) + EPS)
    normed = values * inverse_rms
    return (normed * gain_row, normed, inverse_rms)


def rms_backward(normed, inverse_rms, gain_row, upstream):
    scaled = upstream * gain_row
    through = inverse_rms * (scaled - normed * jnp.mean(scaled * normed, axis=-1, keepdims=True))
    return (through, upstream * normed)


def rotary_tables(positions, head_size):
    half_size = head_size // 2
    inverse_freq = jnp.exp(
        jnp.arange(half_size, dtype=jnp.float32) * (-2.0 * math.log(10000.0) / head_size)
    )
    angles = positions.astype(jnp.float32)[:, None] * inverse_freq[None, :]
    return (jnp.cos(angles), jnp.sin(angles))


def rotate(values, cosine_table, sine_table):
    half_size = values.shape[-1] // 2
    first_half = values[..., :half_size]
    second_half = values[..., half_size:]
    cosine_row = cosine_table[:, None, :]
    sine_row = sine_table[:, None, :]
    return jnp.concatenate(
        [
            first_half * cosine_row - second_half * sine_row,
            second_half * cosine_row + first_half * sine_row,
        ],
        axis=-1,
    )


def gated_gelu(gate_part, up_part):
    return jax.nn.gelu(gate_part, approximate=True) * up_part


def window_mask(query_positions, key_positions):
    query_column = query_positions[:, None]
    key_line = key_positions[None, :]
    return (key_line >= 0) & (key_line <= query_column) & (key_line > query_column - WIN)


def attend(query_block, key_block, value_block, allowed):
    scores = jnp.dot(query_block, key_block.T, preferred_element_type=jnp.float32)
    exponent = jnp.where(allowed, jnp.exp(scores), 0.0)
    totals = jnp.sum(exponent, axis=-1, keepdims=True)
    probabilities = (exponent / totals).astype(jnp.bfloat16)
    mixture = jnp.dot(probabilities, value_block, preferred_element_type=jnp.float32).astype(
        jnp.bfloat16
    )
    return (mixture, jnp.log(totals))


def attend_back(query_block, key_block, value_block, allowed, mixture, log_totals, d_mixture):
    scores = jnp.dot(query_block, key_block.T, preferred_element_type=jnp.float32)
    probabilities = jnp.where(allowed, jnp.exp(scores - log_totals), 0.0)
    delta_row = jnp.sum(
        d_mixture.astype(jnp.float32) * mixture.astype(jnp.float32), axis=-1, keepdims=True
    )
    d_probs = jnp.dot(d_mixture, value_block.T, preferred_element_type=jnp.float32)
    d_scores = (probabilities * (d_probs - delta_row)).astype(jnp.bfloat16)
    d_values = jnp.dot(
        probabilities.astype(jnp.bfloat16).T, d_mixture, preferred_element_type=jnp.float32
    )
    d_queries = jnp.dot(d_scores, key_block, preferred_element_type=jnp.float32)
    d_keys = jnp.dot(d_scores.T, query_block, preferred_element_type=jnp.float32)
    return (d_queries, d_keys, d_values)


MESH = pl.DeviceIdType.MESH


def axis_bits(count):
    return count.bit_length() - 1


def coordinates(bits):
    place = lax.axis_index("seq")
    values = [lax.axis_index("wshard")]
    for bit in range(bits - 1, -1, -1):
        values.append(lax.rem(lax.div(place, 2**bit), 2))
    return values


def partner(dim, coords, bits):
    if dim == 0:
        return (lax.axis_index("seq"), 1 - coords[0])
    step = 2 ** (bits - dim)
    return (lax.axis_index("seq") + (1 - 2 * coords[dim]) * step, lax.axis_index("wshard"))


def greet(coords, bits):
    barrier = pltpu.get_barrier_semaphore()
    for dim in range(bits + 1):
        pl.semaphore_signal(
            barrier, inc=1, device_id=partner(dim, coords, bits), device_id_type=MESH
        )
    pl.semaphore_wait(barrier, bits + 1)


def scatter_order(bits, flipped):
    middle = [0, bits - 1] if flipped else [bits - 1, 0]
    return [bits] + middle + list(range(bits - 2, 0, -1))


class Piece:
    def __init__(self, ref, rows, lanes, wdim, row_part, flipped, dtype=jnp.bfloat16):
        self.ref, self.rows, self.lanes, self.wdim = ref, rows, lanes, wdim
        self.row_part, self.flipped, self.dtype = row_part, flipped, dtype

    def slices(self, picks, bits, base_row):
        index = []
        rows, lanes = pl.ds(base_row, self.rows), pl.ds(0, self.lanes)
        if 0 in picks:
            pick = picks[0]
            if self.wdim == "lead":
                index.append(slice(None) if pick is None else pick)
            else:
                if pick is None:
                    lanes = pl.ds(0, 2 * self.lanes)
                else:
                    lanes = pl.ds(pl.multiple_of(pick * self.lanes, self.lanes), self.lanes)
        for dim in range(1, bits + 1):
            if dim in picks:
                pick = picks[dim]
                index.append(slice(None) if pick is None else pick)
        return tuple(index) + (rows, lanes)

    def shape(self, dims):
        rows, lanes, lead = self.rows, self.lanes, []
        for dim in sorted(dims):
            if dim > 0 or self.wdim == "lead":
                lead.append(2)
            else:
                lanes *= 2
        return tuple(lead) + (rows, lanes)


def make_pieces(shapes):
    out, load = [], [0, 0]
    for number, (rows, lanes, wdim, parts) in enumerate(shapes):
        if rows % (16 * parts):
            parts = 1
        for part in range(parts):
            flipped = load[1] < load[0]
            load[flipped] += rows * lanes // parts
            out.append(Piece(number, rows // parts, lanes, wdim, part, flipped))
    return out


def issue_order(pieces, orders, bits, shrinking):
    free, ready, done = {}, [0.0] * len(pieces), [0] * len(pieces)
    sequence = []
    while len(sequence) < len(pieces) * (bits + 1):
        number = min(
            (n for n in range(len(pieces)) if done[n] <= bits), key=lambda n: (ready[n], done[n], n)
        )
        stage = done[number]
        dim = orders[number][stage]
        blocks = 2 ** (bits - stage) if shrinking else 2**stage
        cost = 0.125 if dim == bits else (2.0 if 0 < dim < bits - 2 else 1.0)
        start = max(ready[number], free.get(dim, 0.0))
        finish = start + blocks * pieces[number].rows * pieces[number].lanes * cost
        free[dim] = ready[number] = finish
        done[number] += 1
        sequence.append((number, stage))
    return sequence


def gather_kernel(pieces, bits, count, *refs):
    blocks, outs = refs[:count], refs[count : 2 * count]
    send_sems, recv_sems, local_sems = refs[2 * count :]
    coords = coordinates(bits)
    own = {dim: coords[dim] for dim in range(bits + 1)}
    local = []
    for number, piece in enumerate(pieces):
        row = piece.row_part * piece.rows
        copy = pltpu.make_async_copy(
            blocks[piece.ref].at[pl.ds(row, piece.rows), :],
            outs[piece.ref].at[piece.slices(own, bits, row)],
            local_sems.at[number],
        )
        copy.start()
        local.append(copy)
    greet(coords, bits)
    orders = [scatter_order(bits, piece.flipped)[::-1] for piece in pieces]
    held = [dict(own) for _ in pieces]
    last = list(local)
    sent = []
    for number, stage in issue_order(pieces, orders, bits, False):
        piece = pieces[number]
        if stage == 0:
            last[number].wait()
        else:
            last[number].wait_recv()
        dim = orders[number][stage]
        row = piece.row_part * piece.rows
        region = outs[piece.ref].at[piece.slices(held[number], bits, row)]
        copy = pltpu.make_async_remote_copy(
            src_ref=region,
            dst_ref=region,
            send_sem=send_sems.at[number, stage],
            recv_sem=recv_sems.at[number, stage],
            device_id=partner(dim, coords, bits),
            device_id_type=MESH,
        )
        copy.start()
        held[number][dim] = None
        last[number] = copy
        sent.append(copy)
    for number in range(len(pieces)):
        last[number].wait_recv()
    for copy in sent:
        copy.wait_send()


def gather_blocks(blocks, shapes, bits):
    pieces = make_pieces(shapes)
    full = []
    for (rows, lanes, wdim, parts), block in zip(shapes, blocks):
        whole = Piece(0, rows, lanes, wdim, 0, False).shape(range(bits + 1))
        full.append(jax.ShapeDtypeStruct(whole, block.dtype))
    count = len(blocks)
    return pl.pallas_call(
        lambda *refs: gather_kernel(pieces, bits, count, *refs),
        out_shape=full,
        in_specs=[pl.BlockSpec(memory_space=pltpu.VMEM)] * count,
        out_specs=[pl.BlockSpec(memory_space=pl.ANY)] * count,
        scratch_shapes=[
            pltpu.SemaphoreType.DMA((len(pieces), bits + 1)),
            pltpu.SemaphoreType.DMA((len(pieces), bits + 1)),
            pltpu.SemaphoreType.DMA((len(pieces),)),
        ],
        compiler_params=pltpu.CompilerParams(collective_id=0, has_side_effects=True),
        name="gather_weights",
    )(*blocks)


def scatter_kernel(pieces, bits, count, *refs):
    grads, outs = refs[:count], refs[count : 2 * count]
    send_sems, recv_sems = refs[-2:]
    slots = refs[2 * count : -2]
    coords = coordinates(bits)
    greet(coords, bits)
    orders = [scatter_order(bits, piece.flipped) for piece in pieces]
    left = [{dim: None for dim in range(bits + 1)} for _ in pieces]
    current = [grads[piece.ref] for piece in pieces]
    rows_at = [piece.row_part * piece.rows for piece in pieces]
    pending = [None] * len(pieces)
    sent = []

    def finish(number, stage, kind):
        copy, keep = pending[number]
        copy.wait_recv()
        slot = slots[number * (bits + 1) + stage]
        mine = current[number][keep].astype(kind)
        total = mine + slot[...].astype(kind)
        current[number], rows_at[number] = slot, 0
        return slot, total

    for number, stage in issue_order(pieces, orders, bits, True):
        piece = pieces[number]
        if stage > 0:
            slot, total = finish(number, stage - 1, current[number].dtype)
            slot[...] = total.astype(slot.dtype)
        dim = orders[number][stage]
        picks = dict(left[number])
        picks[dim] = 1 - coords[dim]
        give = piece.slices(picks, bits, rows_at[number])
        picks[dim] = coords[dim]
        keep = piece.slices(picks, bits, rows_at[number])
        copy = pltpu.make_async_remote_copy(
            src_ref=current[number].at[give],
            dst_ref=slots[number * (bits + 1) + stage],
            send_sem=send_sems.at[number, stage],
            recv_sem=recv_sems.at[number, stage],
            device_id=partner(dim, coords, bits),
            device_id_type=MESH,
        )
        copy.start()
        del left[number][dim]
        pending[number] = (copy, keep)
        sent.append(copy)
    for number, piece in enumerate(pieces):
        slot, total = finish(number, bits, jnp.float32)
        row = piece.row_part * piece.rows
        outs[piece.ref][pl.ds(row, piece.rows), :] = total
    for copy in sent:
        copy.wait_send()


def scatter_blocks(grads, shapes, bits):
    pieces = make_pieces(shapes)
    slots = []
    for piece in pieces:
        dims = list(range(bits + 1))
        for dim in scatter_order(bits, piece.flipped):
            dims.remove(dim)
            slots.append(pltpu.VMEM(piece.shape(dims), grads[piece.ref].dtype))
    count = len(grads)
    return pl.pallas_call(
        lambda *refs: scatter_kernel(pieces, bits, count, *refs),
        out_shape=[
            jax.ShapeDtypeStruct((rows, lanes), jnp.float32) for rows, lanes, _, _ in shapes
        ],
        in_specs=[pl.BlockSpec(memory_space=pltpu.VMEM)] * count,
        out_specs=[pl.BlockSpec(memory_space=pltpu.VMEM)] * count,
        scratch_shapes=slots
        + [
            pltpu.SemaphoreType.DMA((len(pieces), bits + 1)),
            pltpu.SemaphoreType.DMA((len(pieces), bits + 1)),
        ],
        compiler_params=pltpu.CompilerParams(
            collective_id=1, has_side_effects=True, vmem_limit_bytes=60 * 1024 * 1024
        ),
        name="scatter_grads",
    )(*grads)


def shards(block_input, attn_in, attn_out, ffn_in, ffn_out, norm_gains, head_gains, cotangent):
    seq_count = lax.axis_size("seq")
    bits = axis_bits(seq_count)
    gain_rows, gain_cols = norm_gains.shape
    head_rows, head_cols = head_gains.shape
    width = block_input.shape[-1]
    gain_block = jnp.concatenate(
        [
            jnp.pad(norm_gains, ((0, 0), (0, 128 - gain_cols))),
            jnp.pad(head_gains, ((0, 16 - gain_rows - head_rows), (0, 128 - head_cols))),
        ],
        axis=0,
    )
    wide = ffn_in.shape[1] % 256 == 0
    up_block = ffn_in if wide else ffn_in.T
    in_block, out_block, down_block = (attn_in.T, attn_out.T, ffn_out.T)
    layouts = (
        (*in_block.shape, "lead", 2),
        (*out_block.shape, "lanes", 1),
        (*up_block.shape, "lead", 4),
        (*down_block.shape, "lanes", 1),
    )
    gathered = gather_blocks(
        (in_block, out_block, up_block, down_block, gain_block),
        layouts + ((16, 128, "lead", 1),),
        bits,
    )
    in_halves = gathered[0].reshape(2, -1, in_block.shape[1])
    attnin_t = jnp.concatenate([in_halves[0], in_halves[1]], axis=1)
    attnout_t = gathered[1].reshape(width, -1)
    if wide:
        whole_ffnin = (
            gathered[2]
            .reshape(2, seq_count, up_block.shape[0], up_block.shape[1])
            .transpose(0, 2, 1, 3)
            .reshape(width, -1)
        )
    else:
        up_halves = gathered[2].reshape(2, -1, up_block.shape[1])
        whole_ffnin = jnp.concatenate([up_halves[0], up_halves[1]], axis=1).T
    ffnout_t = gathered[3].reshape(width, -1)
    gain_all = gathered[4].reshape(2, seq_count, 16, 128)
    whole_norms = (
        gain_all[:, :, :gain_rows, :gain_cols].transpose(0, 2, 1, 3).reshape(2 * gain_rows, -1)
    )
    whole_heads = (
        gain_all[:, :, gain_rows : gain_rows + head_rows, :head_cols]
        .transpose(0, 2, 1, 3)
        .reshape(2 * head_rows, -1)
    )
    gain_table = whole_norms.astype(jnp.float32)
    head_table = whole_heads.astype(jnp.float32)
    tokens = block_input[0]
    upstream_out = cotangent[0]
    row_count = tokens.shape[0]
    hop_count = (WIN - 1) // row_count + 1
    positions = lax.axis_index("seq") * row_count + jnp.arange(row_count, dtype=jnp.int32)
    normed_in, unit_in, inverse_in = rms_forward(tokens, gain_table[0])
    hidden_in = normed_in.astype(jnp.bfloat16)
    projected = jnp.dot(hidden_in, attnin_t.T, preferred_element_type=jnp.float32)
    query_raw = projected[:, : NQ * HD].reshape(row_count, NQ, HD)
    key_raw = projected[:, NQ * HD : (NQ + 1) * HD].reshape(row_count, 1, HD)
    value_raw = projected[:, (NQ + 1) * HD :]
    query_norm, query_unit, query_inverse = rms_forward(query_raw, head_table[0])
    key_norm, key_unit, key_inverse = rms_forward(key_raw, head_table[1])
    cosine_table, sine_table = rotary_tables(positions, HD)
    query_rot = (
        (rotate(query_norm, cosine_table, sine_table) * QUERY_SCALE)
        .astype(jnp.bfloat16)
        .reshape(row_count * NQ, HD)
    )
    key_rot = rotate(key_norm, cosine_table, sine_table).reshape(row_count, HD).astype(jnp.bfloat16)
    own_pair = jnp.concatenate([key_rot, value_raw.astype(jnp.bfloat16)], axis=1)
    earlier = []
    for distance in range(hop_count, 0, -1):
        earlier.append(shifted(own_pair, "seq", distance))
    window_pair = jnp.concatenate(earlier + [own_pair], axis=0)
    keys_all = window_pair[:, :HD]
    values_all = window_pair[:, HD:]
    key_positions = (
        positions[0]
        - hop_count * row_count
        + jnp.arange((hop_count + 1) * row_count, dtype=jnp.int32)
    )
    allowed = window_mask(jnp.repeat(positions, NQ), key_positions)
    mixture, log_totals = attend(query_rot, keys_all, values_all, allowed)
    attended = mixture.reshape(row_count, NQ * HD)
    attn_proj = jnp.dot(attended, attnout_t.T, preferred_element_type=jnp.float32)
    post_attn, unit_attn, inverse_attn = rms_forward(attn_proj, gain_table[1])
    middle = tokens + post_attn
    normed_mid, unit_mid, inverse_mid = rms_forward(middle, gain_table[2])
    hidden_mid = normed_mid.astype(jnp.bfloat16)
    gate_up = jnp.dot(hidden_mid, whole_ffnin, preferred_element_type=jnp.float32)
    activated, gelu_back = jax.vjp(gated_gelu, gate_up[:, :FF], gate_up[:, FF:])
    activated_bf = activated.astype(jnp.bfloat16)
    ffn_proj = jnp.dot(activated_bf, ffnout_t.T, preferred_element_type=jnp.float32)
    post_ffn, unit_ffn, inverse_ffn = rms_forward(ffn_proj, gain_table[3])
    output = middle + post_ffn
    d_ffnproj, gain_four = rms_backward(unit_ffn, inverse_ffn, gain_table[3], upstream_out)
    d_ffn_bf = d_ffnproj.astype(jnp.bfloat16)
    grad_ffnout = jnp.dot(d_ffn_bf.T, activated_bf, preferred_element_type=jnp.float32)
    d_activated = jnp.dot(d_ffn_bf, ffnout_t, preferred_element_type=jnp.float32)
    d_gate, d_up = gelu_back(d_activated)
    d_gateup = jnp.concatenate([d_gate, d_up], axis=1).astype(jnp.bfloat16)
    grad_ffnin = jnp.dot(hidden_mid.T, d_gateup, preferred_element_type=jnp.float32)
    d_normmid = jnp.dot(d_gateup, whole_ffnin.T, preferred_element_type=jnp.float32)
    d_middle_part, gain_three = rms_backward(unit_mid, inverse_mid, gain_table[2], d_normmid)
    d_middle = upstream_out + d_middle_part
    d_attnproj, gain_two = rms_backward(unit_attn, inverse_attn, gain_table[1], d_middle)
    d_attn_bf = d_attnproj.astype(jnp.bfloat16)
    grad_attnout = jnp.dot(d_attn_bf.T, attended, preferred_element_type=jnp.float32)
    d_mixed = jnp.dot(d_attn_bf, attnout_t, preferred_element_type=jnp.float32).astype(
        jnp.bfloat16
    )
    d_mixed = d_mixed.reshape(row_count * NQ, HD)
    d_queries, d_keys, d_values = attend_back(
        query_rot, keys_all, values_all, allowed, mixture, log_totals, d_mixed
    )
    pair_all = jnp.concatenate([d_keys, d_values], axis=1)
    pair_grad = pair_all[hop_count * row_count :]
    for distance in range(1, hop_count + 1):
        start_row = (hop_count - distance) * row_count
        pair_grad = pair_grad + shifted(
            pair_all[start_row : start_row + row_count].astype(jnp.bfloat16), "seq", -distance
        ).astype(jnp.float32)
    d_keynorm = rotate(pair_grad[:, :HD].reshape(row_count, 1, HD), cosine_table, -sine_table)
    d_keyraw, gain_key = rms_backward(key_unit, key_inverse, head_table[1], d_keynorm)
    d_queryrot = d_queries.reshape(row_count, NQ, HD) * QUERY_SCALE
    d_querynorm = rotate(d_queryrot, cosine_table, -sine_table)
    d_queryraw, gain_query = rms_backward(query_unit, query_inverse, head_table[0], d_querynorm)
    d_projected = jnp.concatenate(
        [
            d_queryraw.reshape(row_count, NQ * HD),
            d_keyraw.reshape(row_count, HD),
            pair_grad[:, HD:],
        ],
        axis=1,
    ).astype(jnp.bfloat16)
    half_width = in_block.shape[1]
    grad_attnin = jnp.stack(
        [
            jnp.dot(
                d_projected.T,
                hidden_in[:, half * half_width : (half + 1) * half_width],
                preferred_element_type=jnp.float32,
            )
            for half in range(2)
        ]
    )
    d_normin = jnp.dot(d_projected, attnin_t, preferred_element_type=jnp.float32)
    d_tokens_part, gain_one = rms_backward(unit_in, inverse_in, gain_table[0], d_normin)
    input_grad = d_middle + d_tokens_part
    grad_norms = jnp.stack(
        [
            jnp.sum(gain_one, axis=0),
            jnp.sum(gain_two, axis=0),
            jnp.sum(gain_three, axis=0),
            jnp.sum(gain_four, axis=0),
        ]
    )
    grad_heads = jnp.stack(
        [jnp.sum(gain_query.reshape(-1, HD), axis=0), jnp.sum(gain_key.reshape(-1, HD), axis=0)]
    )
    bit_dims = (2,) * bits
    gain_sums = jnp.concatenate(
        [
            jnp.pad(
                grad_norms.reshape(2, gain_rows, seq_count, gain_cols).transpose(0, 2, 1, 3),
                ((0, 0), (0, 0), (0, 0), (0, 128 - gain_cols)),
            ),
            jnp.pad(
                grad_heads.reshape(2, head_rows, seq_count, head_cols).transpose(0, 2, 1, 3),
                ((0, 0), (0, 0), (0, 8 - gain_rows - head_rows), (0, 128 - head_cols)),
            ),
        ],
        axis=2,
    )
    up_sums = grad_ffnin.astype(jnp.bfloat16)
    if wide:
        up_sums = (
            up_sums.reshape(2, up_block.shape[0], seq_count, -1)
            .transpose(0, 2, 1, 3)
            .reshape((2,) + bit_dims + up_block.shape)
        )
    else:
        up_sums = up_sums.reshape(2, up_block.shape[1], -1).transpose(0, 2, 1)
        up_sums = up_sums.reshape((2,) + bit_dims + up_block.shape)
    reduced = scatter_blocks(
        (
            grad_attnin.astype(jnp.bfloat16).reshape((2,) + bit_dims + in_block.shape),
            grad_attnout.astype(jnp.bfloat16).reshape(bit_dims + (out_block.shape[0], -1)),
            up_sums,
            grad_ffnout.astype(jnp.bfloat16).reshape(bit_dims + (down_block.shape[0], -1)),
            gain_sums.reshape((2,) + bit_dims + (8, 128)),
        ),
        layouts + ((8, 128, "lead", 1),),
        bits,
    )
    return (
        output[None],
        input_grad[None],
        reduced[0].T,
        reduced[1].T,
        reduced[2] if wide else reduced[2].T,
        reduced[3].T,
        reduced[4][:gain_rows, :gain_cols],
        reduced[4][gain_rows : gain_rows + head_rows, :head_cols],
    )


def solution(mesh):
    in_specs = (
        P("wshard", "seq", None),
        P("wshard", "seq"),
        P("wshard", "seq"),
        P("wshard", "seq"),
        P("wshard", "seq"),
        P("wshard", "seq"),
        P("wshard", "seq"),
        P("wshard", "seq", None),
    )
    out_specs = (
        P("wshard", "seq", None),
        P("wshard", "seq", None),
        P("wshard", "seq"),
        P("wshard", "seq"),
        P("wshard", "seq"),
        P("wshard", "seq"),
        P("wshard", "seq"),
        P("wshard", "seq"),
    )
    return jax.shard_map(shards, mesh=mesh, in_specs=in_specs, out_specs=out_specs, check_vma=False)
```
